256 devices in a mesh: section: 16 (over x, y_lo, core), dp: 8 (over z), tensor: 2 (over y_hi).
Axes of the slice: x: 4, y: 4 (y_hi: 2, y_lo: 2; y = y_hi * 2 + y_lo), z: 8, core: 2. Of those that a mesh axis runs over, the one named last changes fastest.
Arguments:
- activations: bfloat16 [16, 8192, 2048], P('section', 'dp', 'tensor'), may hold values from -150 to 150, as said below
- sent_grads: bfloat16 [16, 8192, 2048], P('section', 'dp', 'tensor'), may hold values from -150 to 150, as said below
- damping: float32 [16, 2, 2], P('section', None, 'tensor'), may hold values from 0.05 to 0.5
- bubble_steps: int32 [16, 2, 2], P('section', None, 'tensor'), may hold values from 1 to 3
- warm: float32 [16, 2, 2, 1024, 1024], P('section', None, 'tensor', 'dp'), may hold values from -0.02 to 1.2, as said below
Outputs:
- inverse: float32 [16, 2, 2, 1024, 1024], P('section', None, 'tensor', 'dp')
The draws below stay inside these ranges and needn't reach their ends.
Inputs may be any that keep to these rules, and one draw needn't show every extreme that they name: `activations`: input features of one section's layer, rows and columns of differing scales. `sent_grads`: gradients of one section's layer outputs, rows and columns of differing scales. `warm`: symmetric with a positive diagonal; Newton-Schulz steps from it contract toward the inverse of each block's factor.
All inputs are finite; a program needn't handle non-finite values.
Results may differ from the reference program's by a relative error of at most 0.0003.
Values may be sent and summed in bfloat16 or wider, within the bound.
A program may use at most 192 MiB of HBM per device.

```python
import math
import jax
import jax.numpy as jnp
from jax import lax

BLOCK = 1024
ITERS = 3
SECTIONS = 16
SPLIT = 2
TOKENS = 8192


def scales(key, salt):
    inner = jax.random.fold_in(key, salt)
    row_key, column_key, value_key = jax.random.split(inner, 3)
    row_scale = jnp.exp(jax.random.uniform(row_key, (SECTIONS, TOKENS), jnp.float32, jnp.log(0.5), jnp.log(5.0)))
    column_scale = jnp.exp(jax.random.uniform(column_key, (SECTIONS, SPLIT * BLOCK), jnp.float32, jnp.log(0.5), jnp.log(5.0)))
    return (row_scale, column_scale, value_key)


def scaled_values(key, salt):
    row_scale, column_scale, value_key = scales(key, salt)
    shape = (SECTIONS, TOKENS, SPLIT * BLOCK)
    values = jax.random.truncated_normal(value_key, -6.0, 6.0, shape, jnp.float32)
    return values * row_scale[:, :, None] * column_scale[:, None, :]


def draw_activations(key, part):
    return scaled_values(key, 11).astype(jnp.bfloat16)


def draw_sent_grads(key, part):
    return scaled_values(key, 12).astype(jnp.bfloat16)


def diagonal_of(key, salt, roll):
    row_scale, column_scale, value_key = scales(key, salt)
    mean_square = jnp.mean(row_scale * row_scale, axis=1)
    diag = column_scale * column_scale * mean_square[:, None]
    if roll:
        diag = jnp.roll(diag, -1, axis=0)
    return diag.reshape(SECTIONS, SPLIT, BLOCK)


def draw_warm(key, part):
    diags = jnp.stack([diagonal_of(key, 11, False), diagonal_of(key, 12, True)], axis=1)
    noise_key = jax.random.fold_in(key, 13)
    noise = 0.003 * jax.random.truncated_normal(noise_key, -6.0, 6.0, (SECTIONS, 2, SPLIT, BLOCK, BLOCK), jnp.float32)
    noise = 0.5 * (noise + jnp.swapaxes(noise, -1, -2))
    middle = 0.77 * (jnp.eye(BLOCK, dtype=jnp.float32) + noise)
    root = 1.0 / jnp.sqrt(diags)
    return middle * root[..., :, None] * root[..., None, :]


def place_ends(result, stream_key, low, largest):
    longest = result.shape.index(max(result.shape))
    spots = []
    for shift in (0, 1):
        where = [jax.random.randint(jax.random.fold_in(stream_key, axis), (), 0, length) for axis, length in enumerate(result.shape)]
        where[longest] = (where[longest] + shift) % result.shape[longest]
        spots.append(tuple(where))
    return result.at[spots[0]].set(low).at[spots[1]].set(largest)


def steps_of(stream_key, extent, pieces, least, top_value):
    def one(dim, parts):
        heights = jax.random.uniform(jax.random.fold_in(jax.random.fold_in(stream_key, 6), dim), (parts,), jnp.float32, least / len(pieces), top_value / len(pieces))
        return jnp.repeat(jnp.exp(heights), extent[dim] // parts).reshape((-1,) + (1,) * (len(extent) - dim - 1))

    level = one(*pieces[0])
    for cut in pieces[1:]:
        level = level * one(*cut)
    return level


def setup_inputs(seed: int = 0) -> dict:
    streams_of = jax.random.split(jax.random.key(seed), 6)
    activations = draw_activations(jax.random.fold_in(streams_of[5], 71), 0)
    sent_grads = draw_sent_grads(jax.random.fold_in(streams_of[5], 71), 0)
    damping = jnp.clip(jnp.exp(math.log(0.5) - 2.3025851 * jax.random.uniform(streams_of[2], (SECTIONS, 2, SPLIT), jnp.float32) ** steps_of(streams_of[2], (SECTIONS, 2, SPLIT), ((0, 16), (2, 2)), -0.2, 0.2)), 0.05, 0.5)
    bubble_steps = place_ends(jax.random.randint(streams_of[3], (SECTIONS, 2, SPLIT), 1, ITERS + 1), jax.random.fold_in(streams_of[3], 1), 1, ITERS).astype(jnp.int32)
    warm = draw_warm(jax.random.fold_in(streams_of[5], 71), 0)
    return dict(activations=activations, sent_grads=sent_grads, damping=damping, bubble_steps=bubble_steps, warm=warm)


def gram(rows):
    return lax.dot_general(rows, rows, (((0,), (0,)), ((), ())), preferred_element_type=jnp.float32)


def refine(factor, start, count):
    iterate = start
    for index in range(ITERS):
        product = jnp.dot(iterate, factor, precision=lax.Precision.HIGHEST)
        updated = 2.0 * iterate - jnp.dot(product, iterate, precision=lax.Precision.HIGHEST)
        iterate = jnp.where(index < count, updated, iterate)
    return iterate


def reference(activations, sent_grads, damping, bubble_steps, warm):
    identity = jnp.eye(BLOCK, dtype=jnp.float32)

    def one_section(section):
        nxt = jnp.minimum(section + 1, SECTIONS - 1).astype(jnp.int32)
        keep = (section + 1 < SECTIONS).astype(jnp.float32)
        inputs = activations[section]
        received = (sent_grads[nxt].astype(jnp.float32) * keep).astype(jnp.bfloat16)
        blocks = []
        for kind in range(2):
            source = inputs if kind == 0 else received
            row = []
            for split in range(SPLIT):
                rows = source[:, split * BLOCK:(split + 1) * BLOCK]
                factor = gram(rows) / TOKENS + damping[section, kind, split] * identity
                row.append(refine(factor, warm[section, kind, split], bubble_steps[section, kind, split]))
            blocks.append(jnp.stack(row))
        return jnp.stack(blocks)

    return lax.map(one_section, jnp.arange(SECTIONS, dtype=jnp.int32))
```

```python
import functools

import jax
import jax.numpy as jnp
from jax import lax
from jax.experimental import pallas as pl
from jax.experimental.pallas import tpu as pltpu
from jax.sharding import PartitionSpec as P

MESH = pl.DeviceIdType.MESH
ITERS = 3
RING = 8
ROWS = 128
STRIP = 5
WIDE = STRIP * ROWS
HALF = ROWS // 2
LEVELS = 32767.0
TINY = 1e-30


def diagonal_mask():
    row = lax.broadcasted_iota(jnp.int32, (ROWS, ROWS), 0)
    column = lax.broadcasted_iota(jnp.int32, (ROWS, ROWS), 1)
    return row == column


def encode(strip, code_ref, side_ref):
    mask = diagonal_mask()
    square = strip[:, :ROWS]
    diagonal = jnp.where(mask, square, 0.0)
    along_lanes = jnp.sum(diagonal, axis=0, keepdims=True)
    along_rows = jnp.sum(diagonal, axis=1, keepdims=True)
    rest = jnp.concatenate([jnp.where(mask, 0.0, square), strip[:, ROWS:]], axis=1)
    scaled = rest / jnp.sqrt(jnp.maximum(along_rows, TINY))
    largest = jnp.maximum(jnp.max(jnp.abs(scaled), axis=0, keepdims=True), TINY)
    code_ref[...] = jnp.round(scaled * (LEVELS / largest)).astype(jnp.int32).astype(jnp.int16)
    largest = largest / LEVELS
    pieces = [largest[:, b * ROWS:(b + 1) * ROWS] for b in range(STRIP)]
    zero = jnp.zeros_like(along_lanes)
    side_ref[...] = jnp.concatenate(pieces + [along_lanes, zero, zero], axis=0)


def exchange_kernel(act, grad, warm, fs, fd, xs, xd, a, g, rb, qb, qd, in_sem, rs_send, rs_recv, ag_send, ag_recv, hop_sem):
    z = lax.axis_index("dp")
    s = lax.axis_index("section")
    sections = lax.axis_size("section")
    right, left = lax.rem(z + 1, RING), lax.rem(z + RING - 1, RING)
    before, behind = lax.rem(s + sections - 1, sections), lax.rem(s + 1, sections)
    width = act.shape[1]
    extra = WIDE - ROWS

    loads = []
    for m, source in enumerate((act, grad)):
        loads.append((
            pltpu.make_async_copy(source, a.at[m, :, pl.ds(0, width)], in_sem.at[m, 0]),
            pltpu.make_async_copy(source.at[:, pl.ds(0, extra)], a.at[m, :, pl.ds(width, extra)], in_sem.at[m, 1]),
        ))
        for copy in loads[-1]:
            copy.start()

    barrier = pltpu.get_barrier_semaphore()
    for target in ({"dp": right}, {"dp": left}, {"section": before}, {"section": behind}):
        pl.semaphore_signal(barrier, inc=1, device_id=target, device_id_type=MESH)

    for m in range(2):
        blocks = [
            warm[m, :, pl.ds(pl.multiple_of(lax.rem(z + b, RING) * ROWS, ROWS), ROWS)] for b in range(STRIP)
        ]
        encode(jnp.concatenate(blocks, axis=1), xs.at[m, z], xd.at[m, z])
    pl.semaphore_wait(barrier, 4)

    sent = []

    def start(copy):
        copy.start()
        sent.append(copy)

    def gram(m, owner):
        first = pl.multiple_of(owner * ROWS, ROWS)
        g[m, owner] = lax.dot_general(
            a[m, :, pl.ds(first, ROWS)], a[m, :, pl.ds(first, WIDE)],
            (((0,), (0,)), ((), ())), preferred_element_type=jnp.float32,
        )

    def reduce_copy(m, d, step, source):
        return pltpu.make_async_remote_copy(
            src_ref=source, dst_ref=rb.at[m, d, step], send_sem=rs_send.at[m, d, step], recv_sem=rs_recv.at[m, d, step],
            device_id={"dp": (right, left)[d]}, device_id_type=MESH,
        )

    def gather_copies(which, codes, sides, m, d, step, owner):
        rows = (pl.ds(0, ROWS), pl.ds(d * HALF, HALF))[step == RING // 2 - 1]
        target = {"dp": (right, left)[d]}
        code = codes.at[m, owner, rows]
        copies = [pltpu.make_async_remote_copy(
            src_ref=code, dst_ref=code, send_sem=ag_send.at[which, m, d, step, 0], recv_sem=ag_recv.at[which, m, d, step, 0],
            device_id=target, device_id_type=MESH,
        )]
        if step < RING // 2 - 1 or d == 0:
            side = sides.at[m, owner]
            copies.append(pltpu.make_async_remote_copy(
                src_ref=side, dst_ref=side, send_sem=ag_send.at[which, m, d, step, 1], recv_sem=ag_recv.at[which, m, d, step, 1],
                device_id=target, device_id_type=MESH,
            ))
        return copies

    def owner_of(d, distance):
        return lax.rem(z + (RING - distance, distance)[d], RING)

    def gather_start(which, codes, sides, m, step):
        for d in range(2):
            for copy in gather_copies(which, codes, sides, m, d, step, owner_of(d, step)):
                start(copy)

    def gather_wait(which, codes, sides, m, step):
        for d in range(2):
            for copy in gather_copies(which, codes, sides, m, d, step, owner_of(d, step + 1)):
                copy.wait_recv()

    for m in range(2):
        for copy in loads[m]:
            copy.wait()
        for d in range(2):
            owner = owner_of(d, 1)
            gram(m, owner)
            start(reduce_copy(m, d, 0, g.at[m, owner, pl.ds(d * HALF, HALF)]))
    for m in range(2):
        gather_start(0, xs, xd, m, 0)

    @pl.loop(0, RING - 2)
    def _(j):
        owner = lax.rem(z + 2 + j + j // (RING - 3), RING)
        for m in range(2):
            gram(m, owner)

    for step in range(RING - 1):
        for m in (1, 0):
            for d in range(2):
                slot = rb.at[m, d, step]
                reduce_copy(m, d, step, slot).wait_recv()
                owner = owner_of(d, (step + 2) % RING)
                slot[...] += g[m, owner, pl.ds(d * HALF, HALF)]
                if step < RING - 2:
                    start(reduce_copy(m, d, step + 1, slot))
        if step < RING // 2:
            for m in range(2):
                gather_wait(0, xs, xd, m, step)
                if step < RING // 2 - 1:
                    gather_start(0, xs, xd, m, step + 1)

    tokens = act.shape[0] * RING

    def total(m):
        return jnp.concatenate([rb[m, 0, RING - 2], rb[m, 1, RING - 2]], axis=0) * (1.0 / tokens)

    encode(total(1), qb, qd)
    qd[...] = jnp.where(s > 0, qd[...], 0.0)
    hops = [
        pltpu.make_async_remote_copy(
            src_ref=source, dst_ref=target, send_sem=hop_sem.at[0, i], recv_sem=hop_sem.at[1, i],
            device_id={"section": before}, device_id_type=MESH,
        )
        for i, (source, target) in enumerate(((qb, fs.at[1, z]), (qd, fd.at[1, z])))
    ]
    for copy in hops:
        start(copy)
    encode(total(0), fs.at[0, z], fd.at[0, z])
    gather_start(1, fs, fd, 0, 0)
    for copy in hops:
        copy.wait_recv()
    gather_start(1, fs, fd, 1, 0)
    for step in range(RING // 2):
        for m in range(2):
            gather_wait(1, fs, fd, m, step)
            if step < RING // 2 - 1:
                gather_start(1, fs, fd, m, step + 1)
    for copy in sent:
        copy.wait_send()


def exchange(act, grad, warm):
    tokens, width = act.shape
    code = jax.ShapeDtypeStruct((2, RING, ROWS, WIDE), jnp.int16)
    side = jax.ShapeDtypeStruct((2, RING, 8, ROWS), jnp.float32)
    whole = pl.BlockSpec(memory_space=pltpu.VMEM)
    return pl.pallas_call(
        exchange_kernel,
        out_shape=(code, side, code, side),
        in_specs=[pl.BlockSpec(memory_space=pl.ANY), pl.BlockSpec(memory_space=pl.ANY), whole],
        out_specs=(whole,) * 4,
        scratch_shapes=[
            pltpu.VMEM((2, tokens, width + WIDE - ROWS), jnp.bfloat16),
            pltpu.VMEM((2, RING, ROWS, WIDE), jnp.float32),
            pltpu.VMEM((2, 2, RING - 1, HALF, WIDE), jnp.float32),
            pltpu.VMEM((ROWS, WIDE), jnp.int16),
            pltpu.VMEM((8, ROWS), jnp.float32),
            pltpu.SemaphoreType.DMA((2, 2)),
            pltpu.SemaphoreType.DMA((2, 2, RING - 1)),
            pltpu.SemaphoreType.DMA((2, 2, RING - 1)),
            pltpu.SemaphoreType.DMA((2, 2, 2, RING // 2, 2)),
            pltpu.SemaphoreType.DMA((2, 2, 2, RING // 2, 2)),
            pltpu.SemaphoreType.DMA((2, 2)),
        ],
        compiler_params=pltpu.CompilerParams(collective_id=0, has_side_effects=True, vmem_limit_bytes=60 << 20),
        name="exchange",
    )(act, grad, warm)


def split(value):
    high = value.astype(jnp.bfloat16)
    return high, (value - high.astype(jnp.float32)).astype(jnp.bfloat16)


def decode(code_ref, side_ref, shift, high_ref, low_ref):
    mask = diagonal_mask()

    @pl.loop(0, RING)
    def _(o):
        side = side_ref[o]
        diagonal = side[STRIP:STRIP + 1]
        root = jnp.sqrt(jnp.maximum(jnp.sum(jnp.where(mask, diagonal, 0.0), axis=1, keepdims=True), TINY))
        rows = pl.ds(pl.multiple_of(o * ROWS, ROWS), ROWS)
        for b in range(STRIP):
            block = code_ref[o, :, pl.ds(b * ROWS, ROWS)].astype(jnp.int32).astype(jnp.float32)
            block = block * side[b:b + 1] * root
            if b == 0:
                block = jnp.where(mask, diagonal + shift, block)
            high, low = split(block)
            columns = pl.ds(pl.multiple_of(lax.rem(o + b, RING) * ROWS, ROWS), ROWS)
            high_ref[rows, columns] = high
            low_ref[rows, columns] = low
            if 0 < b < STRIP - 1:
                high_ref[columns, rows] = high.T
                low_ref[columns, rows] = low.T


def refine_kernel(damping, counts, warm, fs, fd, xs, xd, out, fh, fl, xh, xl, ys, ts, y):
    m = pl.program_id(0)
    decode(xs.at[0], xd.at[0], 0.0, xh, xl)
    decode(fs.at[0], fd.at[0], damping[m], fh, fl)
    width = y.shape[1]
    tile = 256

    def put(ref, columns, value):
        high, low = split(value)
        ref[pl.ds(0, ROWS), columns] = high
        ref[pl.ds(ROWS, ROWS), columns] = low

    def product(left, high_ref, low_ref, columns):
        both = jnp.dot(left[...], high_ref[:, columns], preferred_element_type=jnp.float32)
        cross = jnp.dot(left[pl.ds(0, ROWS)], low_ref[:, columns], preferred_element_type=jnp.float32)
        return both[:ROWS] + (both[ROWS:] + cross)

    out[0] = warm[0]
    y[...] = warm[0]
    put(ys, pl.ds(0, width), warm[0])
    for index in range(ITERS):
        @pl.loop(0, 2 ** index)
        def _(_i):
            @pl.loop(0, width // tile)
            def _(j):
                columns = pl.ds(pl.multiple_of(j * tile, tile), tile)
                put(ts, columns, product(ys, fh, fl, columns))

            @pl.loop(0, width // tile)
            def _(j):
                columns = pl.ds(pl.multiple_of(j * tile, tile), tile)
                y[:, columns] = y[:, columns] - product(ts, xh, xl, columns)

            put(ys, pl.ds(0, width), y[...])

        advanced = out[0] + y[...]
        out[0] = jnp.where(index < counts[m], advanced, out[0])
        if index < ITERS - 1:
            y[...] = out[0]
            put(ys, pl.ds(0, width), out[0])


def refine(damping, counts, warm, fs, fd, xs, xd):
    width = warm.shape[2]
    scalar = pl.BlockSpec(memory_space=pltpu.SMEM)
    rows = pl.BlockSpec((1, ROWS, width), lambda m: (m, 0, 0))
    code = pl.BlockSpec((1, RING, ROWS, WIDE), lambda m: (m, 0, 0, 0))
    side = pl.BlockSpec((1, RING, 8, ROWS), lambda m: (m, 0, 0, 0))
    full = pltpu.VMEM((width, width), jnp.bfloat16)
    return pl.pallas_call(
        refine_kernel,
        grid=(2,),
        out_shape=jax.ShapeDtypeStruct(warm.shape, jnp.float32),
        in_specs=[scalar, scalar, rows, code, side, code, side],
        out_specs=rows,
        scratch_shapes=[full] * 4 + [pltpu.VMEM((2 * ROWS, width), jnp.bfloat16)] * 2 + [pltpu.VMEM((ROWS, width), jnp.float32)],
        compiler_params=pltpu.CompilerParams(vmem_limit_bytes=60 << 20),
        name="refine",
    )(damping, counts, warm, fs, fd, xs, xd)


def local(activations, sent_grads, damping, bubble_steps, warm):
    rows = warm[0, :, 0]
    codes = exchange(activations[0], sent_grads[0], rows)
    return refine(damping[0, :, 0], bubble_steps[0, :, 0], rows, *codes)[None, :, None]


def solution(mesh):
    placed = (
        P("section", "dp", "tensor"),
        P("section", "dp", "tensor"),
        P("section", None, "tensor"),
        P("section", None, "tensor"),
        P("section", None, "tensor", "dp", None),
    )
    return jax.shard_map(
        local,
        mesh=mesh,
        in_specs=placed,
        out_specs=P("section", None, "tensor", "dp", None),
        check_vma=False,
    )
```

```python
import functools

import jax
import jax.numpy as jnp
from jax import lax
from jax.experimental import pallas as pl
from jax.experimental.pallas import tpu as pltpu
from jax.sharding import PartitionSpec as P

MESH = pl.DeviceIdType.MESH
ITERS = 3
RING = 8
ROWS = 128
STRIP = 5
WIDE = STRIP * ROWS
HALF = ROWS // 2
LEVELS = 32767.0
TINY = 1e-30


def diagonal_mask(rows, first):
    row = lax.broadcasted_iota(jnp.int32, (rows, ROWS), 0) + first
    column = lax.broadcasted_iota(jnp.int32, (rows, ROWS), 1)
    return row == column


def encode(strip, code_ref, side_ref, first=0):
    mask = diagonal_mask(strip.shape[0], first)
    square = strip[:, :ROWS]
    diagonal = jnp.where(mask, square, 0.0)
    along_lanes = jnp.sum(diagonal, axis=0, keepdims=True)
    along_rows = jnp.sum(diagonal, axis=1, keepdims=True)
    rest = jnp.concatenate([jnp.where(mask, 0.0, square), strip[:, ROWS:]], axis=1)
    scaled = rest / jnp.sqrt(jnp.maximum(along_rows, TINY))
    largest = jnp.maximum(jnp.max(jnp.abs(scaled), axis=0, keepdims=True), TINY)
    code_ref[...] = jnp.round(scaled * (LEVELS / largest)).astype(jnp.int32).astype(jnp.int16)
    largest = largest / LEVELS
    pieces = [largest[:, b * ROWS:(b + 1) * ROWS] for b in range(STRIP)]
    zero = jnp.zeros_like(along_lanes)
    side_ref[...] = jnp.concatenate(pieces + [along_lanes, zero, zero], axis=0)


def decode(code, side, first=0, shift=0.0):
    rows = code.shape[0]
    mask = diagonal_mask(rows, first)
    diagonal = side[STRIP:STRIP + 1]
    root = jnp.sqrt(jnp.maximum(jnp.sum(jnp.where(mask, diagonal, 0.0), axis=1, keepdims=True), TINY))
    blocks = []
    for b in range(STRIP):
        block = code[:, b * ROWS:(b + 1) * ROWS].astype(jnp.int32).astype(jnp.float32) * side[b:b + 1] * root
        if b == 0:
            block = jnp.where(mask, diagonal + shift, block)
        blocks.append(block)
    return blocks


def split(value):
    high = value.astype(jnp.bfloat16)
    return high, (value - high.astype(jnp.float32)).astype(jnp.bfloat16)


def kernel(
    damping, counts, act, grad, warm, out,
    a, g, rb, rside, xs, xd, fs, fd, qb, qd, full, ys, ts, y,
    in_sem, rs_send, rs_recv, ag_send, ag_recv, hop_sem,
):
    z = lax.axis_index("dp")
    s = lax.axis_index("section")
    sections = lax.axis_size("section")
    right, left = lax.rem(z + 1, RING), lax.rem(z + RING - 1, RING)
    before, behind = lax.rem(s + sections - 1, sections), lax.rem(s + 1, sections)
    width = act.shape[1]
    extra = WIDE - ROWS
    tokens = act.shape[0] * RING
    last_step = RING // 2 - 1
    last_hop = RING - 2
    sent = []

    def start(copies):
        for copy in copies:
            copy.start()
            sent.append(copy)

    def remote(source, target, send, receive, device):
        return pltpu.make_async_remote_copy(
            src_ref=source, dst_ref=target, send_sem=send, recv_sem=receive, device_id=device, device_id_type=MESH,
        )

    def owner_of(d, distance):
        return lax.rem(z + (RING - distance, distance)[d], RING)

    def half(d):
        return pl.ds(d * HALF, HALF)

    def gram(m, owner):
        first = pl.multiple_of(owner * ROWS, ROWS)
        g[m, owner] = lax.dot_general(
            a[m, :, pl.ds(first, ROWS)], a[m, :, pl.ds(first, WIDE)],
            (((0,), (0,)), ((), ())), preferred_element_type=jnp.float32,
        )

    def reduce_copies(m, d, hop, source):
        device = {"dp": (right, left)[d]}
        return [
            remote(ref.at[m, d, source], ref.at[m, d, hop], rs_send.at[m, d, hop, i], rs_recv.at[m, d, hop, i], device)
            for i, ref in enumerate((rb, rside))
        ]

    def reduce_first(m):
        for d in range(2):
            owner = owner_of(d, 1)
            gram(m, owner)
            encode(g[m, owner, half(d)], rb.at[m, d, RING - 1], rside.at[m, d, RING - 1], d * HALF)

    def reduce_start(m):
        for d in range(2):
            start(reduce_copies(m, d, 0, RING - 1))

    def gram_rest(m):
        @pl.loop(0, RING - 2)
        def _(j):
            gram(m, lax.rem(z + 2 + j + j // (RING - 3), RING))

    def reduce_hop(m, hop):
        for d in range(2):
            for copy in reduce_copies(m, d, hop, hop):
                copy.wait_recv()
            owner = owner_of(d, (hop + 2) % RING)
            received = jnp.concatenate(decode(rb[m, d, hop], rside[m, d, hop], d * HALF), axis=1)
            value = received + g[m, owner, half(d)]
            if hop < last_hop:
                encode(value, rb.at[m, d, hop], rside.at[m, d, hop], d * HALF)
                start(reduce_copies(m, d, hop + 1, hop))
            else:
                g[m, owner, half(d)] = value * (1.0 / tokens)

    stores = ((xs, xd), (fs, fd))

    def gather_copies(which, m, d, step, owner):
        codes, sides = stores[which]
        rows = half(d) if step == last_step else pl.ds(0, ROWS)
        pairs = [codes.at[m, owner, rows]]
        if step < last_step or d == 0:
            pairs.append(sides.at[m, owner])
        return [
            remote(ref, ref, ag_send.at[which, m, d, step, i], ag_recv.at[which, m, d, step, i], {"dp": (right, left)[d]})
            for i, ref in enumerate(pairs)
        ]

    def gather_start(which, m, step):
        for d in range(2):
            start(gather_copies(which, m, d, step, owner_of(d, step)))

    def gather_step(which, m, step):
        for d in range(2):
            for copy in gather_copies(which, m, d, step, owner_of(d, step + 1)):
                copy.wait_recv()
        if step < last_step:
            gather_start(which, m, step + 1)

    def spread(which, m, owner):
        codes, sides = stores[which]
        shift = (0.0, damping[m])[which]
        high_ref, low_ref = full.at[which, m, 0], full.at[which, m, 1]
        rows = pl.ds(pl.multiple_of(owner * ROWS, ROWS), ROWS)
        for b, block in enumerate(decode(codes[m, owner], sides[m, owner], 0, shift)):
            high, low = split(block)
            columns = pl.ds(pl.multiple_of(lax.rem(owner + b, RING) * ROWS, ROWS), ROWS)
            high_ref[rows, columns] = high
            low_ref[rows, columns] = low
            if 0 < b < STRIP - 1:
                high_ref[columns, rows] = high.T
                low_ref[columns, rows] = low.T

    def spread_step(which, m, step):
        if step == last_step:
            spread(which, m, owner_of(1, step + 1))
        else:
            @pl.loop(0, 2)
            def _(d):
                spread(which, m, lax.rem(z + RING + (2 * d - 1) * (step + 1), RING))

    tile = 512

    def put(ref, columns, value):
        high, low = split(value)
        ref[pl.ds(0, ROWS), columns] = high
        ref[pl.ds(ROWS, ROWS), columns] = low

    def product(rows, which, m, columns):
        both = jnp.dot(rows[...], full[which, m, 0, :, columns], preferred_element_type=jnp.float32)
        cross = jnp.dot(rows[pl.ds(0, ROWS)], full[which, m, 1, :, columns], preferred_element_type=jnp.float32)
        return both[:ROWS] + (both[ROWS:] + cross)

    def begin(m):
        out[m] = warm[m]
        y[...] = warm[m]
        put(ys, pl.ds(0, width), warm[m])

    def by_factor(m):
        @pl.loop(0, width // tile)
        def _(j):
            columns = pl.ds(pl.multiple_of(j * tile, tile), tile)
            put(ts, columns, product(ys, 1, m, columns))

    def by_inverse(m, index, last):
        @pl.loop(0, width // tile)
        def _(j):
            columns = pl.ds(pl.multiple_of(j * tile, tile), tile)
            value = y[:, columns] - product(ts, 0, m, columns)
            if last:
                old = out[m, :, columns]
                value = jnp.where(index < counts[m], old + value, old)
                out[m, :, columns] = value
            y[:, columns] = value
            put(ys, columns, value)

    loads = []
    for m, source in enumerate((act, grad)):
        loads.append((
            pltpu.make_async_copy(source, a.at[m, :, pl.ds(0, width)], in_sem.at[m, 0]),
            pltpu.make_async_copy(source.at[:, pl.ds(0, extra)], a.at[m, :, pl.ds(width, extra)], in_sem.at[m, 1]),
        ))
        for copy in loads[-1]:
            copy.start()

    barrier = pltpu.get_barrier_semaphore()
    for target in ({"dp": right}, {"dp": left}, {"section": before}, {"section": behind}):
        pl.semaphore_signal(barrier, inc=1, device_id=target, device_id_type=MESH)

    for m in range(2):
        blocks = [
            warm[m, :, pl.ds(pl.multiple_of(lax.rem(z + b, RING) * ROWS, ROWS), ROWS)] for b in range(STRIP)
        ]
        encode(jnp.concatenate(blocks, axis=1), xs.at[m, z], xd.at[m, z])

    for copy in loads[0]:
        copy.wait()
    reduce_first(0)
    pl.semaphore_wait(barrier, 4)
    reduce_start(0)
    gather_start(0, 0, 0)
    gram_rest(0)
    for copy in loads[1]:
        copy.wait()
    reduce_first(1)
    gram_rest(1)

    for hop in range(last_hop + 1):
        reduce_hop(0, hop)
        if hop <= last_step:
            gather_step(0, 0, hop)
        if hop == 2:
            reduce_start(1)
        if hop == last_hop:
            encode(g[0, z], fs.at[0, z], fd.at[0, z])
            gather_start(1, 0, 0)
        if hop >= 3:
            reduce_hop(1, hop - 3)
        if hop == 3:
            spread(0, 0, z)
        elif hop > 3:
            spread_step(0, 0, hop - 4)

    hops = [
        remote(source, target, hop_sem.at[0, i], hop_sem.at[1, i], {"section": before})
        for i, (source, target) in enumerate(((qb, fs.at[1, z]), (qd, fd.at[1, z])))
    ]
    spread(1, 0, z)
    spread_step(0, 0, last_step)
    for step in range(last_step + 1):
        gather_step(1, 0, step)
        if step < last_step:
            reduce_hop(1, step + last_hop - 2)
        if step == last_step - 1:
            encode(g[1, z], qb, qd)
            qd[...] = jnp.where(s > 0, qd[...], 0.0)
            start(hops)
            gather_start(0, 1, 0)
        spread_step(1, 0, step)

    def arrive():
        for copy in hops:
            copy.wait_recv()
        gather_start(1, 1, 0)
        spread(0, 1, z)
        spread(1, 1, z)

    def advance(which, step):
        gather_step(which, 1, step)
        spread_step(which, 1, step)

    events = [None, arrive]
    for step in range(last_step + 1):
        events += [functools.partial(advance, 0, step), None, functools.partial(advance, 1, step)]
    events = iter(events)

    def event():
        do = next(events, None)
        if do is not None:
            do()

    begin(0)
    for index in range(ITERS):
        for i in range(2 ** index):
            by_factor(0)
            event()
            by_inverse(0, index, i == 2 ** index - 1)
            event()
    for do in events:
        if do is not None:
            do()

    begin(1)
    for index in range(ITERS):
        if index:
            @pl.loop(0, 2 ** index - 1)
            def _(_i):
                by_factor(1)
                by_inverse(1, index, False)
        by_factor(1)
        by_inverse(1, index, True)

    for copy in sent:
        copy.wait_send()


def run(damping, counts, act, grad, warm):
    tokens, width = act.shape
    whole = pl.BlockSpec(memory_space=pltpu.VMEM)
    scalar = pl.BlockSpec(memory_space=pltpu.SMEM)
    code = pltpu.VMEM((2, RING, ROWS, WIDE), jnp.int16)
    side = pltpu.VMEM((2, RING, 8, ROWS), jnp.float32)
    return pl.pallas_call(
        kernel,
        out_shape=jax.ShapeDtypeStruct(warm.shape, jnp.float32),
        in_specs=[scalar, scalar, pl.BlockSpec(memory_space=pl.ANY), pl.BlockSpec(memory_space=pl.ANY), whole],
        out_specs=whole,
        scratch_shapes=[
            pltpu.VMEM((2, tokens, width + WIDE - ROWS), jnp.bfloat16),
            pltpu.VMEM((2, RING, ROWS, WIDE), jnp.float32),
            pltpu.VMEM((2, 2, RING, HALF, WIDE), jnp.int16),
            pltpu.VMEM((2, 2, RING, 8, ROWS), jnp.float32),
            code, side, code, side,
            pltpu.VMEM((ROWS, WIDE), jnp.int16),
            pltpu.VMEM((8, ROWS), jnp.float32),
            pltpu.VMEM((2, 2, 2, width, width), jnp.bfloat16),
            pltpu.VMEM((2 * ROWS, width), jnp.bfloat16),
            pltpu.VMEM((2 * ROWS, width), jnp.bfloat16),
            pltpu.VMEM((ROWS, width), jnp.float32),
            pltpu.SemaphoreType.DMA((2, 2)),
            pltpu.SemaphoreType.DMA((2, 2, RING - 1, 2)),
            pltpu.SemaphoreType.DMA((2, 2, RING - 1, 2)),
            pltpu.SemaphoreType.DMA((2, 2, 2, RING // 2, 2)),
            pltpu.SemaphoreType.DMA((2, 2, 2, RING // 2, 2)),
            pltpu.SemaphoreType.DMA((2, 2)),
        ],
        compiler_params=pltpu.CompilerParams(collective_id=0, has_side_effects=True, vmem_limit_bytes=62 << 20),
        name="factors",
    )(damping, counts, act, grad, warm)


def local(activations, sent_grads, damping, bubble_steps, warm):
    refined = run(damping[0, :, 0], bubble_steps[0, :, 0], activations[0], sent_grads[0], warm[0, :, 0])
    return refined[None, :, None]


def solution(mesh):
    placed = (
        P("section", "dp", "tensor"),
        P("section", "dp", "tensor"),
        P("section", None, "tensor"),
        P("section", None, "tensor"),
        P("section", None, "tensor", "dp", None),
    )
    return jax.shard_map(
        local,
        mesh=mesh,
        in_specs=placed,
        out_specs=P("section", None, "tensor", "dp", None),
        check_vma=False,
    )
```

```python
import functools

import jax
import jax.numpy as jnp
from jax import lax
from jax.experimental import pallas as pl
from jax.experimental.pallas import tpu as pltpu
from jax.sharding import PartitionSpec as P

MESH = pl.DeviceIdType.MESH
ITERS = 3
RING = 8
ROWS = 128
STRIP = 5
WIDE = STRIP * ROWS
HALF = ROWS // 2
LEVELS = 32767.0
TINY = 1e-30


def diagonal_mask(rows, first):
    row = lax.broadcasted_iota(jnp.int32, (rows, ROWS), 0) + first
    column = lax.broadcasted_iota(jnp.int32, (rows, ROWS), 1)
    return row == column


def encode(strip, code_ref, side_ref, h):
    mask = diagonal_mask(HALF, h * HALF)
    square = strip[:, :ROWS]
    diagonal = jnp.where(mask, square, 0.0)
    along_lanes = jnp.sum(diagonal, axis=0, keepdims=True)
    along_rows = jnp.sum(diagonal, axis=1, keepdims=True)
    rest = jnp.concatenate([jnp.where(mask, 0.0, square), strip[:, ROWS:]], axis=1)
    scaled = rest * (1.0 / jnp.sqrt(jnp.maximum(along_rows, TINY)))
    largest = jnp.maximum(jnp.max(jnp.abs(scaled), axis=0, keepdims=True), TINY)
    code_ref[...] = jnp.round(scaled * (LEVELS / largest)).astype(jnp.int32).astype(jnp.int16)
    largest = largest / LEVELS
    pieces = [largest[:, b * ROWS:(b + 1) * ROWS] for b in range(STRIP - h)]
    zero = jnp.zeros_like(along_lanes)
    side_ref[...] = jnp.concatenate(pieces + [zero] * h + [along_lanes, zero, zero], axis=0)


def decode(code, side, h, shift=0.0):
    mask = diagonal_mask(HALF, h * HALF)
    diagonal = side[STRIP:STRIP + 1]
    root = jnp.sqrt(jnp.maximum(jnp.sum(jnp.where(mask, diagonal, 0.0), axis=1, keepdims=True), TINY))
    blocks = []
    for b in range(STRIP - h):
        block = code[:, b * ROWS:(b + 1) * ROWS].astype(jnp.int32).astype(jnp.float32) * side[b:b + 1] * root
        if b == 0:
            block = jnp.where(mask, diagonal + shift, block)
        blocks.append(block)
    return blocks


def left_lanes():
    return lax.broadcasted_iota(jnp.int32, (HALF, ROWS), 1) < HALF


def halves(strip):
    lower = strip[HALF:]
    corner = pltpu.roll(lower[:, WIDE - ROWS:], HALF, 1)
    corners = jnp.where(left_lanes(), corner, lower[:, :ROWS])
    return strip[:HALF], jnp.concatenate([corners, lower[:, ROWS:WIDE - ROWS]], axis=1)


def split(value):
    high = value.astype(jnp.bfloat16)
    return high, (value - high.astype(jnp.float32)).astype(jnp.bfloat16)


def kernel(
    damping, counts, act, grad, warm, out,
    a, g0, g1, r0, r1, rside, x0, x1, xd, f0, f1, fd, q0, q1, qd, full, ys, ts, y,
    in_sem, rs_send, rs_recv, ag_send, ag_recv, hop_sem,
):
    z = lax.axis_index("dp")
    s = lax.axis_index("section")
    sections = lax.axis_size("section")
    right, left = lax.rem(z + 1, RING), lax.rem(z + RING - 1, RING)
    before, behind = lax.rem(s + sections - 1, sections), lax.rem(s + 1, sections)
    width = act.shape[1]
    extra = WIDE - ROWS
    tokens = act.shape[0] * RING
    last_step = RING // 2 - 1
    last_hop = RING - 2
    early = 0
    sent = []

    def start(copies):
        for copy in copies:
            copy.start()
            sent.append(copy)

    def remote(source, target, send, receive, device):
        return pltpu.make_async_remote_copy(
            src_ref=source, dst_ref=target, send_sem=send, recv_sem=receive, device_id=device, device_id_type=MESH,
        )

    def owner_of(d, distance):
        return lax.rem(z + (RING - distance, distance)[d], RING)

    g, rb, xs, fs, qb = (g0, g1), (r0, r1), (x0, x1), (f0, f1), (q0, q1)

    def gram(m, owner):
        first = pl.multiple_of(owner * ROWS, ROWS)
        strip = lax.dot_general(
            a[m, :, pl.ds(first, ROWS)], a[m, :, pl.ds(first, WIDE)],
            (((0,), (0,)), ((), ())), preferred_element_type=jnp.float32,
        )
        for h, value in enumerate(halves(strip)):
            g[h][m, owner] = value

    def reduce_copies(m, d, hop, source):
        device = {"dp": (right, left)[d]}
        pairs = ((rb[d ^ m].at[m, source], rb[d ^ m].at[m, hop]), (rside.at[m, d, source], rside.at[m, d, hop]))
        return [
            remote(a_ref, b_ref, rs_send.at[m, d, hop, i], rs_recv.at[m, d, hop, i], device)
            for i, (a_ref, b_ref) in enumerate(pairs)
        ]

    def reduce_start(m):
        for d in range(2):
            start(reduce_copies(m, d, 0, RING - 1))

    def reduce_hop(m, hop):
        for d in range(2):
            h = d ^ m
            for copy in reduce_copies(m, d, hop, hop):
                copy.wait_recv()
            owner = owner_of(d, (hop + 2) % RING)
            received = jnp.concatenate(decode(rb[h][m, hop], rside[m, d, hop], h), axis=1)
            value = received + g[h][m, owner]
            if hop < last_hop:
                encode(value, rb[h].at[m, hop], rside.at[m, d, hop], h)
                start(reduce_copies(m, d, hop + 1, hop))
            else:
                g[h][m, owner] = value * (1.0 / tokens)

    stores = ((xs, xd), (fs, fd))

    def gather_copies(which, m, d, step, h, owner):
        codes, sides = stores[which]
        return [
            remote(ref, ref, ag_send.at[which, m, d, step, h, i], ag_recv.at[which, m, d, step, h, i], {"dp": (right, left)[d]})
            for i, ref in enumerate((codes[h].at[m, owner], sides.at[m, h, owner]))
        ]

    def gather_start(which, m):
        for h in range(2):
            for d in range(2):
                start(gather_copies(which, m, d, 0, h ^ d, owner_of(d, 0)))

    def gather_turn(which, m, count):
        step, turn = count // 2, count % 2
        for d in range(2):
            h = turn ^ d
            owner = owner_of(d, step + 1)
            for copy in gather_copies(which, m, d, step, h, owner):
                copy.wait_recv()
            if step + 1 + turn <= last_step:
                start(gather_copies(which, m, d, step + 1, h, owner))

    def spread(which, m, owner):
        codes, sides = stores[which]
        shift = (0.0, damping[m])[which]
        upper, lower = (decode(codes[h][m, owner], sides[m, h, owner], h, shift) for h in range(2))
        far = lax.rem(owner + STRIP - 1, RING)
        left = left_lanes()
        empty = jnp.zeros((HALF, ROWS), jnp.float32)

        def store(block, row_block, column_block, bottom):
            columns = pl.ds(pl.multiple_of(column_block * ROWS, ROWS), ROWS)
            rows = pl.ds(pl.multiple_of(row_block * ROWS + bottom * HALF, HALF), block.shape[0])
            for i, part in enumerate(split(block)):
                full[which, m, i, rows, columns] = part

        def merge(block, row_block, column_block, mask):
            columns = pl.ds(pl.multiple_of(column_block * ROWS, ROWS), ROWS)
            rows = pl.ds(pl.multiple_of(row_block * ROWS + HALF, HALF), HALF)
            for i, part in enumerate(split(block)):
                old = full[which, m, i, rows, columns].astype(jnp.float32)
                full[which, m, i, rows, columns] = jnp.where(mask, part.astype(jnp.float32), old).astype(jnp.bfloat16)

        flipped = jnp.concatenate([upper[0], empty], axis=0).T
        store(jnp.concatenate([upper[0], jnp.where(left, flipped[HALF:], lower[0])], axis=0), owner, owner, 0)
        for b in range(1, STRIP - 1):
            block = jnp.concatenate([upper[b], lower[b]], axis=0)
            other = lax.rem(owner + b, RING)
            store(block, owner, other, 0)
            store(block.T, other, owner, 0)
        store(upper[STRIP - 1], owner, far, 0)
        merge(pltpu.roll(lower[0], HALF, 1), owner, far, jnp.logical_not(left))
        merge(jnp.concatenate([upper[STRIP - 1], empty], axis=0).T[HALF:], far, owner, left)

    def spread_step(which, m, step):
        if step == last_step:
            spread(which, m, owner_of(1, step + 1))
        else:
            @pl.loop(0, 2)
            def _(d):
                spread(which, m, lax.rem(z + RING + (2 * d - 1) * (step + 1), RING))

    tile = 512

    def put(ref, columns, value):
        high, low = split(value)
        ref[pl.ds(0, ROWS), columns] = high
        ref[pl.ds(ROWS, ROWS), columns] = low

    def product(rows, which, m, columns):
        both = jnp.dot(rows[...], full[which, m, 0, :, columns], preferred_element_type=jnp.float32)
        cross = jnp.dot(rows[pl.ds(0, ROWS)], full[which, m, 1, :, columns], preferred_element_type=jnp.float32)
        return both[:ROWS] + (both[ROWS:] + cross)

    def begin(m):
        out[m] = warm[m]
        y[...] = warm[m]
        put(ys, pl.ds(0, width), warm[m])

    def by_factor(m):
        @pl.loop(0, width // tile)
        def _(j):
            columns = pl.ds(pl.multiple_of(j * tile, tile), tile)
            put(ts, columns, product(ys, 1, m, columns))

    def by_inverse(m, index, last):
        @pl.loop(0, width // tile)
        def _(j):
            columns = pl.ds(pl.multiple_of(j * tile, tile), tile)
            value = y[:, columns] - product(ts, 0, m, columns)
            if last:
                old = out[m, :, columns]
                value = jnp.where(index < counts[m], old + value, old)
                out[m, :, columns] = value * 0.5 if index == ITERS - 1 else value
            y[:, columns] = value
            put(ys, columns, value)

    loads = []
    for m, source in enumerate((act, grad)):
        loads.append((
            pltpu.make_async_copy(source, a.at[m, :, pl.ds(0, width)], in_sem.at[m, 0]),
            pltpu.make_async_copy(source.at[:, pl.ds(0, extra)], a.at[m, :, pl.ds(width, extra)], in_sem.at[m, 1]),
        ))
        for copy in loads[-1]:
            copy.start()

    barrier = pltpu.get_barrier_semaphore()
    for target in ({"dp": right}, {"dp": left}, {"section": before}, {"section": behind}):
        pl.semaphore_signal(barrier, inc=1, device_id=target, device_id_type=MESH)

    for m in range(2):
        blocks = [
            warm[m, :, pl.ds(pl.multiple_of(lax.rem(z + b, RING) * ROWS, ROWS), ROWS)] for b in range(STRIP)
        ]
        for h, value in enumerate(halves(jnp.concatenate(blocks, axis=1))):
            encode(value, xs[h].at[m, z], xd.at[m, h, z], h)

    pl.semaphore_wait(barrier, 4)
    gather_start(0, 0)
    for m in range(2):
        for copy in loads[m]:
            copy.wait()
        for d in range(2):
            owner = owner_of(d, 1)
            gram(m, owner)
            encode(g[d ^ m][m, owner], rb[d ^ m].at[m, RING - 1], rside.at[m, d, RING - 1], d ^ m)
        reduce_start(m)

    hops = [
        remote(source, target, hop_sem.at[0, i], hop_sem.at[1, i], {"section": before})
        for i, (source, target) in enumerate((
            (q0, f0.at[1, z]), (q1, f1.at[1, z]), (qd.at[0], fd.at[1, 0, z]), (qd.at[1], fd.at[1, 1, z]),
        ))
    ]
    turns = RING - 1

    def turned(which, m, count):
        gather_turn(which, m, count)
        if count == turns - 1:
            spread_step(which, m, last_step)
        elif count % 2:
            spread_step(which, m, count // 2)

    slots = [functools.partial(turned, 0, 0, count) for count in range(turns)]
    slots += [functools.partial(gather_start, 0, 1)] + [functools.partial(turned, 0, 1, count) for count in range(early)]
    slots = iter(slots)
    for hop in range(last_hop + 1):
        for m in range(2):
            if hop < 2:
                gram(m, owner_of(0, hop + 2))
                gram(m, owner_of(1, hop + 2))
            elif hop < 4:
                gram(m, owner_of(0, (hop + 2, RING)[hop - 2]))
            reduce_hop(m, hop)
            if hop == last_hop and m == 0:
                for h in range(2):
                    encode(g[h][0, z], fs[h].at[0, z], fd.at[0, h, z], h)
                gather_start(1, 0)
            do = next(slots, None)
            if do is not None:
                do()
    for h in range(2):
        encode(g[h][1, z], qb[h], qd.at[h], h)
    qd[...] = jnp.where(s > 0, qd[...], 0.0)
    start(hops)
    for do in slots:
        do()
    spread(0, 0, z)
    spread(1, 0, z)
    for count in range(turns):
        turned(1, 0, count)
        if count == turns - 3:
            for copy in hops:
                copy.wait_recv()
            gather_start(1, 1)
    spread(0, 1, z)
    spread(1, 1, z)

    rest = [functools.partial(turned, 0, 1, count) for count in range(early, turns)]
    main = [functools.partial(turned, 1, 1, count) for count in range(turns)]
    waiting = []
    for i in range(turns):
        waiting += main[i:i + 1] + rest[i:i + 1]
    products = 2 * (2 ** ITERS - 1)
    events = [[] for _ in range(products)]
    for i, do in enumerate(waiting):
        events[(i + 1) * products // len(waiting) - 1].append(do)
    events = iter(events)

    def event():
        for do in next(events):
            do()

    begin(0)
    for index in range(ITERS):
        for i in range(2 ** index):
            by_factor(0)
            event()
            by_inverse(0, index, i == 2 ** index - 1)
            event()
    begin(1)
    for index in range(ITERS):
        if index:
            @pl.loop(0, 2 ** index - 1)
            def _(_i):
                by_factor(1)
                by_inverse(1, index, False)
        by_factor(1)
        by_inverse(1, index, True)

    for copy in sent:
        copy.wait_send()


def run(damping, counts, act, grad, warm):
    tokens, width = act.shape
    whole = pl.BlockSpec(memory_space=pltpu.VMEM)
    scalar = pl.BlockSpec(memory_space=pltpu.SMEM)
    def pair(shape, dtype):
        return [pltpu.VMEM(shape + (HALF, WIDE - h * ROWS), dtype) for h in range(2)]

    side = pltpu.VMEM((2, 2, RING, 8, ROWS), jnp.float32)
    return pl.pallas_call(
        kernel,
        out_shape=jax.ShapeDtypeStruct(warm.shape, jnp.float32),
        in_specs=[scalar, scalar, pl.BlockSpec(memory_space=pl.ANY), pl.BlockSpec(memory_space=pl.ANY), whole],
        out_specs=whole,
        scratch_shapes=[
            pltpu.VMEM((2, tokens, width + WIDE - ROWS), jnp.bfloat16),
            *pair((2, RING), jnp.float32),
            *pair((2, RING), jnp.int16),
            side,
            *pair((2, RING), jnp.int16),
            side,
            *pair((2, RING), jnp.int16),
            side,
            *pair((), jnp.int16),
            pltpu.VMEM((2, 8, ROWS), jnp.float32),
            pltpu.VMEM((2, 2, 2, width, width), jnp.bfloat16),
            pltpu.VMEM((2 * ROWS, width), jnp.bfloat16),
            pltpu.VMEM((2 * ROWS, width), jnp.bfloat16),
            pltpu.VMEM((ROWS, width), jnp.float32),
            pltpu.SemaphoreType.DMA((2, 2)),
            pltpu.SemaphoreType.DMA((2, 2, RING - 1, 2)),
            pltpu.SemaphoreType.DMA((2, 2, RING - 1, 2)),
            pltpu.SemaphoreType.DMA((2, 2, 2, RING // 2, 2, 2)),
            pltpu.SemaphoreType.DMA((2, 2, 2, RING // 2, 2, 2)),
            pltpu.SemaphoreType.DMA((2, 4)),
        ],
        compiler_params=pltpu.CompilerParams(collective_id=0, has_side_effects=True, vmem_limit_bytes=62 << 20),
        name="factors",
    )(damping, counts, act, grad, warm)


def local(activations, sent_grads, damping, bubble_steps, warm):
    refined = run(damping[0, :, 0], bubble_steps[0, :, 0], activations[0], sent_grads[0], warm[0, :, 0])
    return (2.0 * refined)[None, :, None]


def solution(mesh):
    placed = (
        P("section", "dp", "tensor"),
        P("section", "dp", "tensor"),
        P("section", None, "tensor"),
        P("section", None, "tensor"),
        P("section", None, "tensor", "dp", None),
    )
    return jax.shard_map(
        local,
        mesh=mesh,
        in_specs=placed,
        out_specs=P("section", None, "tensor", "dp", None),
        check_vma=False,
    )
```

```python
import functools

import jax
import jax.numpy as jnp
from jax import lax
from jax.experimental import pallas as pl
from jax.experimental.pallas import tpu as pltpu
from jax.sharding import PartitionSpec as P

MESH = pl.DeviceIdType.MESH
ITERS = 3
RING = 8
ROWS = 128
STRIP = 5
WIDE = STRIP * ROWS
HALF = ROWS // 2
LEVELS = 32767.0
TINY = 1e-30


def diagonal_mask(rows, first):
    row = lax.broadcasted_iota(jnp.int32, (rows, ROWS), 0) + first
    column = lax.broadcasted_iota(jnp.int32, (rows, ROWS), 1)
    return row == column


def encode(strip, code_ref, side_ref, h):
    mask = diagonal_mask(HALF, h * HALF)
    square = strip[:, :ROWS]
    diagonal = jnp.where(mask, square, 0.0)
    along_lanes = jnp.sum(diagonal, axis=0, keepdims=True)
    along_rows = jnp.sum(diagonal, axis=1, keepdims=True)
    rest = jnp.concatenate([jnp.where(mask, 0.0, square), strip[:, ROWS:]], axis=1)
    scaled = rest * (1.0 / jnp.sqrt(jnp.maximum(along_rows, TINY)))
    largest = jnp.maximum(jnp.max(jnp.abs(scaled), axis=0, keepdims=True), TINY)
    code_ref[...] = jnp.round(scaled * (LEVELS / largest)).astype(jnp.int32).astype(jnp.int16)
    largest = largest / LEVELS
    pieces = [largest[:, b * ROWS:(b + 1) * ROWS] for b in range(STRIP - h)]
    zero = jnp.zeros_like(along_lanes)
    side_ref[...] = jnp.concatenate(pieces + [zero] * h + [along_lanes, zero, zero], axis=0)


def decode(code, side, h, shift=0.0):
    mask = diagonal_mask(HALF, h * HALF)
    diagonal = side[STRIP:STRIP + 1]
    root = jnp.sqrt(jnp.maximum(jnp.sum(jnp.where(mask, diagonal, 0.0), axis=1, keepdims=True), TINY))
    blocks = []
    for b in range(STRIP - h):
        block = code[:, b * ROWS:(b + 1) * ROWS].astype(jnp.int32).astype(jnp.float32) * side[b:b + 1] * root
        if b == 0:
            block = jnp.where(mask, diagonal + shift, block)
        blocks.append(block)
    return blocks


def left_lanes():
    return lax.broadcasted_iota(jnp.int32, (HALF, ROWS), 1) < HALF


def halves(strip):
    lower = strip[HALF:]
    corner = pltpu.roll(lower[:, WIDE - ROWS:], HALF, 1)
    corners = jnp.where(left_lanes(), corner, lower[:, :ROWS])
    return strip[:HALF], jnp.concatenate([corners, lower[:, ROWS:WIDE - ROWS]], axis=1)


def split(value):
    high = value.astype(jnp.bfloat16)
    return high, (value - high.astype(jnp.float32)).astype(jnp.bfloat16)


def kernel(
    damping, counts, act, grad, warm, out,
    a, g0, g1, r0, r1, rside, x0, x1, xd, f0, f1, fd, q0, q1, qd, full, ys, ts, y,
    in_sem, rs_send, rs_recv, ag_send, ag_recv, hop_sem,
):
    z = lax.axis_index("dp")
    s = lax.axis_index("section")
    sections = lax.axis_size("section")
    right, left = lax.rem(z + 1, RING), lax.rem(z + RING - 1, RING)
    before, behind = lax.rem(s + sections - 1, sections), lax.rem(s + 1, sections)
    width = act.shape[1]
    extra = WIDE - ROWS
    tokens = act.shape[0] * RING
    last_step = RING // 2 - 1
    last_hop = RING - 2
    early = 0
    sent = []

    def start(copies):
        for copy in copies:
            copy.start()
            sent.append(copy)

    def remote(source, target, send, receive, device):
        return pltpu.make_async_remote_copy(
            src_ref=source, dst_ref=target, send_sem=send, recv_sem=receive, device_id=device, device_id_type=MESH,
        )

    def owner_of(d, distance):
        return lax.rem(z + (RING - distance, distance)[d], RING)

    g, rb, xs, fs, qb = (g0, g1), (r0, r1), (x0, x1), (f0, f1), (q0, q1)

    def gram(m, owner):
        first = pl.multiple_of(owner * ROWS, ROWS)
        strip = lax.dot_general(
            a[m, :, pl.ds(first, ROWS)], a[m, :, pl.ds(first, WIDE)],
            (((0,), (0,)), ((), ())), preferred_element_type=jnp.float32,
        )
        for h, value in enumerate(halves(strip)):
            g[h][m, owner] = value

    def reduce_copies(m, d, hop, source):
        device = {"dp": (right, left)[d]}
        pairs = ((rb[d ^ m].at[m, source], rb[d ^ m].at[m, hop]), (rside.at[m, d, source], rside.at[m, d, hop]))
        return [
            remote(a_ref, b_ref, rs_send.at[m, d, hop, i], rs_recv.at[m, d, hop, i], device)
            for i, (a_ref, b_ref) in enumerate(pairs)
        ]

    def reduce_start(m):
        for d in range(2):
            start(reduce_copies(m, d, 0, RING - 1))

    def reduce_hop(m, hop):
        for d in range(2):
            h = d ^ m
            for copy in reduce_copies(m, d, hop, hop):
                copy.wait_recv()
            owner = owner_of(d, (hop + 2) % RING)
            received = jnp.concatenate(decode(rb[h][m, hop], rside[m, d, hop], h), axis=1)
            value = received + g[h][m, owner]
            if hop < last_hop:
                encode(value, rb[h].at[m, hop], rside.at[m, d, hop], h)
                start(reduce_copies(m, d, hop + 1, hop))
            else:
                g[h][m, owner] = value * (1.0 / tokens)

    stores = ((xs, xd), (fs, fd))

    def gather_copies(which, m, d, step, h, owner):
        codes, sides = stores[which]
        return [
            remote(ref, ref, ag_send.at[which, m, d, step, h, i], ag_recv.at[which, m, d, step, h, i], {"dp": (right, left)[d]})
            for i, ref in enumerate((codes[h].at[m, owner], sides.at[m, h, owner]))
        ]

    def gather_start(which, m):
        for h in range(2):
            for d in range(2):
                start(gather_copies(which, m, d, 0, h ^ d, owner_of(d, 0)))

    def gather_turn(which, m, count):
        step, turn = count // 2, count % 2
        for d in range(2):
            h = turn ^ d
            owner = owner_of(d, step + 1)
            for copy in gather_copies(which, m, d, step, h, owner):
                copy.wait_recv()
            if step + 1 + turn <= last_step:
                start(gather_copies(which, m, d, step + 1, h, owner))

    def spread(which, m, owner):
        codes, sides = stores[which]
        shift = (0.0, damping[m])[which]
        upper, lower = (decode(codes[h][m, owner], sides[m, h, owner], h, shift) for h in range(2))
        far = lax.rem(owner + STRIP - 1, RING)
        left = left_lanes()
        empty = jnp.zeros((HALF, ROWS), jnp.float32)

        def store(block, row_block, column_block, bottom):
            columns = pl.ds(pl.multiple_of(column_block * ROWS, ROWS), ROWS)
            rows = pl.ds(pl.multiple_of(row_block * ROWS + bottom * HALF, HALF), block.shape[0])
            for i, part in enumerate(split(block)):
                full[which, m, i, rows, columns] = part

        def merge(block, row_block, column_block, mask):
            columns = pl.ds(pl.multiple_of(column_block * ROWS, ROWS), ROWS)
            rows = pl.ds(pl.multiple_of(row_block * ROWS + HALF, HALF), HALF)
            for i, part in enumerate(split(block)):
                old = full[which, m, i, rows, columns].astype(jnp.float32)
                full[which, m, i, rows, columns] = jnp.where(mask, part.astype(jnp.float32), old).astype(jnp.bfloat16)

        flipped = jnp.concatenate([upper[0], empty], axis=0).T
        store(jnp.concatenate([upper[0], jnp.where(left, flipped[HALF:], lower[0])], axis=0), owner, owner, 0)
        for b in range(1, STRIP - 1):
            block = jnp.concatenate([upper[b], lower[b]], axis=0)
            other = lax.rem(owner + b, RING)
            store(block, owner, other, 0)
            store(block.T, other, owner, 0)
        store(upper[STRIP - 1], owner, far, 0)
        merge(pltpu.roll(lower[0], HALF, 1), owner, far, jnp.logical_not(left))
        merge(jnp.concatenate([upper[STRIP - 1], empty], axis=0).T[HALF:], far, owner, left)

    def spread_step(which, m, step):
        if step == last_step:
            spread(which, m, owner_of(1, step + 1))
        else:
            @pl.loop(0, 2)
            def _(d):
                spread(which, m, lax.rem(z + RING + (2 * d - 1) * (step + 1), RING))

    tile = 512

    def put(ref, columns, value):
        high, low = split(value)
        ref[pl.ds(0, ROWS), columns] = high
        ref[pl.ds(ROWS, ROWS), columns] = low

    def product(rows, which, m, columns):
        both = jnp.dot(rows[...], full[which, m, 0, :, columns], preferred_element_type=jnp.float32)
        cross = jnp.dot(rows[pl.ds(0, ROWS)], full[which, m, 1, :, columns], preferred_element_type=jnp.float32)
        return both[:ROWS] + (both[ROWS:] + cross)

    def begin(m):
        out[m] = warm[m]
        y[...] = warm[m]
        put(ys, pl.ds(0, width), warm[m])

    def by_factor(m):
        @pl.loop(0, width // tile)
        def _(j):
            columns = pl.ds(pl.multiple_of(j * tile, tile), tile)
            put(ts, columns, product(ys, 1, m, columns))

    def by_inverse(m, index, last):
        @pl.loop(0, width // tile)
        def _(j):
            columns = pl.ds(pl.multiple_of(j * tile, tile), tile)
            value = y[:, columns] - product(ts, 0, m, columns)
            if last:
                old = out[m, :, columns]
                value = jnp.where(index < counts[m], old + value, old)
                out[m, :, columns] = value * 0.5 if index == ITERS - 1 else value
            y[:, columns] = value
            put(ys, columns, value)

    loads = []
    for m, source in enumerate((act, grad)):
        loads.append((
            pltpu.make_async_copy(source, a.at[m, :, pl.ds(0, width)], in_sem.at[m, 0]),
            pltpu.make_async_copy(source.at[:, pl.ds(0, extra)], a.at[m, :, pl.ds(width, extra)], in_sem.at[m, 1]),
        ))
        for copy in loads[-1]:
            copy.start()

    barrier = pltpu.get_barrier_semaphore()
    for target in ({"dp": right}, {"dp": left}, {"section": before}, {"section": behind}):
        pl.semaphore_signal(barrier, inc=1, device_id=target, device_id_type=MESH)

    for m in range(2):
        blocks = [
            warm[m, :, pl.ds(pl.multiple_of(lax.rem(z + b, RING) * ROWS, ROWS), ROWS)] for b in range(STRIP)
        ]
        for h, value in enumerate(halves(jnp.concatenate(blocks, axis=1))):
            encode(value, xs[h].at[m, z], xd.at[m, h, z], h)

    pl.semaphore_wait(barrier, 4)
    gather_start(0, 0)
    for m in range(2):
        for copy in loads[m]:
            copy.wait()
        for d in range(2):
            owner = owner_of(d, 1)
            gram(m, owner)
            encode(g[d ^ m][m, owner], rb[d ^ m].at[m, RING - 1], rside.at[m, d, RING - 1], d ^ m)
        reduce_start(m)

    hops = [
        remote(source, target, hop_sem.at[0, i], hop_sem.at[1, i], {"section": before})
        for i, (source, target) in enumerate((
            (q0, f0.at[1, z]), (q1, f1.at[1, z]), (qd.at[0], fd.at[1, 0, z]), (qd.at[1], fd.at[1, 1, z]),
        ))
    ]
    turns = RING - 1

    def turned(which, m, count):
        gather_turn(which, m, count)
        if count == turns - 1:
            spread_step(which, m, last_step)
        elif count % 2:
            spread_step(which, m, count // 2)

    slots = [functools.partial(turned, 0, 0, count) for count in range(turns)]
    slots += [functools.partial(gather_start, 0, 1)] + [functools.partial(turned, 0, 1, count) for count in range(early)]
    slots = iter(slots)
    for hop in range(last_hop + 1):
        for m in range(2):
            if hop < 2:
                gram(m, owner_of(0, hop + 2))
                gram(m, owner_of(1, hop + 2))
            elif hop < 4:
                gram(m, owner_of(0, (hop + 2, RING)[hop - 2]))
            reduce_hop(m, hop)
            if hop == last_hop and m == 0:
                for h in range(2):
                    encode(g[h][0, z], fs[h].at[0, z], fd.at[0, h, z], h)
                gather_start(1, 0)
            if m == 1 or hop < 2:
                do = next(slots, None)
                if do is not None:
                    do()
    for h in range(2):
        encode(g[h][1, z], qb[h], qd.at[h], h)
    qd[...] = jnp.where(s > 0, qd[...], 0.0)
    start(hops)
    for do in slots:
        do()
    spread(0, 0, z)
    spread(1, 0, z)
    for count in range(turns):
        turned(1, 0, count)
        if count == turns - 3:
            for copy in hops:
                copy.wait_recv()
            gather_start(1, 1)
    spread(0, 1, z)
    spread(1, 1, z)

    rest = [functools.partial(turned, 0, 1, count) for count in range(early, turns)]
    main = [functools.partial(turned, 1, 1, count) for count in range(turns)]
    waiting = []
    for i in range(turns):
        waiting += main[i:i + 1] + rest[i:i + 1]
    products = 2 * (2 ** ITERS - 1)
    events = [[] for _ in range(products)]
    for i, do in enumerate(waiting):
        events[(i + 1) * products // len(waiting) - 1].append(do)
    events = iter(events)

    def event():
        for do in next(events):
            do()

    begin(0)
    for index in range(ITERS):
        for i in range(2 ** index):
            by_factor(0)
            event()
            by_inverse(0, index, i == 2 ** index - 1)
            event()
    begin(1)
    for index in range(ITERS):
        if index:
            @pl.loop(0, 2 ** index - 1)
            def _(_i):
                by_factor(1)
                by_inverse(1, index, False)
        by_factor(1)
        by_inverse(1, index, True)

    for copy in sent:
        copy.wait_send()


def run(damping, counts, act, grad, warm):
    tokens, width = act.shape
    whole = pl.BlockSpec(memory_space=pltpu.VMEM)
    scalar = pl.BlockSpec(memory_space=pltpu.SMEM)
    def pair(shape, dtype):
        return [pltpu.VMEM(shape + (HALF, WIDE - h * ROWS), dtype) for h in range(2)]

    side = pltpu.VMEM((2, 2, RING, 8, ROWS), jnp.float32)
    return pl.pallas_call(
        kernel,
        out_shape=jax.ShapeDtypeStruct(warm.shape, jnp.float32),
        in_specs=[scalar, scalar, pl.BlockSpec(memory_space=pl.ANY), pl.BlockSpec(memory_space=pl.ANY), whole],
        out_specs=whole,
        scratch_shapes=[
            pltpu.VMEM((2, tokens, width + WIDE - ROWS), jnp.bfloat16),
            *pair((2, RING), jnp.float32),
            *pair((2, RING), jnp.int16),
            side,
            *pair((2, RING), jnp.int16),
            side,
            *pair((2, RING), jnp.int16),
            side,
            *pair((), jnp.int16),
            pltpu.VMEM((2, 8, ROWS), jnp.float32),
            pltpu.VMEM((2, 2, 2, width, width), jnp.bfloat16),
            pltpu.VMEM((2 * ROWS, width), jnp.bfloat16),
            pltpu.VMEM((2 * ROWS, width), jnp.bfloat16),
            pltpu.VMEM((ROWS, width), jnp.float32),
            pltpu.SemaphoreType.DMA((2, 2)),
            pltpu.SemaphoreType.DMA((2, 2, RING - 1, 2)),
            pltpu.SemaphoreType.DMA((2, 2, RING - 1, 2)),
            pltpu.SemaphoreType.DMA((2, 2, 2, RING // 2, 2, 2)),
            pltpu.SemaphoreType.DMA((2, 2, 2, RING // 2, 2, 2)),
            pltpu.SemaphoreType.DMA((2, 4)),
        ],
        compiler_params=pltpu.CompilerParams(collective_id=0, has_side_effects=True, vmem_limit_bytes=62 << 20),
        name="factors",
    )(damping, counts, act, grad, warm)


def local(activations, sent_grads, damping, bubble_steps, warm):
    refined = run(damping[0, :, 0], bubble_steps[0, :, 0], activations[0], sent_grads[0], warm[0, :, 0])
    return (2.0 * refined)[None, :, None]


def solution(mesh):
    placed = (
        P("section", "dp", "tensor"),
        P("section", "dp", "tensor"),
        P("section", None, "tensor"),
        P("section", None, "tensor"),
        P("section", None, "tensor", "dp", None),
    )
    return jax.shard_map(
        local,
        mesh=mesh,
        in_specs=placed,
        out_specs=P("section", None, "tensor", "dp", None),
        check_vma=False,
    )
```
